512 devices in a mesh: blk: 512 (over y, z, x, core).
Axes of the slice: x: 4, y: 4, z: 16, core: 2. Of those that a mesh axis runs over, the one named last changes fastest.
Arguments:
- geometry: float32 [8, 524288], P(None, 'blk'), may hold values from -1 to 89.333333, as said below
- currents: float32 [32, 524288], P(None, 'blk'), may hold values from -6 to 6
- net_ids: int32 [524288], P('blk'), may hold values from 0 to 3
- pair_on: int32 [512, 8], P('blk'), may hold values from 0 to 1, as said below
Outputs:
- voltage: float32 [32, 524288], P(None, 'blk')
The draws below stay inside these ranges and needn't reach their ends.
Inputs may be any that keep to these rules, and one draw needn't show every extreme that they name: `geometry`: rows 0 to 1 lie in 0 to 512 / 6 + 4, row 2 in 0 to 0.2, rows 3 to 5 form a unit vector, row 6 lies in 0.2 to 2 and row 7 in 0.05 to 0.5. Symmetric: pair_on[b, 4 + d - 1] equals pair_on[(b + d) mod 512, d - 1] for d = 1 .. 4.
All inputs are finite; a program needn't handle non-finite values.
Results may differ from the reference program's by a relative error of at most 0.0003.
Values sent between devices are 32-bit elements; how exact they have to be, the bound alone decides.
No kernel may reach another device: no remote copies, remote signals or barrier semaphores. Data moves between devices by JAX's collectives and lax.ppermute only.
A program may use at most 64 MiB of HBM per device.

```python
import jax
import jax.numpy as jnp
from jax import lax

SEG_DEV = 1024
COLS = 32
REACH = 4
NETS = 4
SEGMENTS = 524288
N_BLK = 512


def draw_geometry(key, part):
    keys = jax.random.split(jax.random.fold_in(key, 11), 7)
    count = SEGMENTS
    spacing = 0.5
    loop_radius = N_BLK * spacing / (2.0 * jnp.pi)
    block_index = (jnp.arange(count, dtype=jnp.int32) // SEG_DEV).astype(jnp.float32)
    theta = 2.0 * jnp.pi * block_index / N_BLK
    centre_x = 2.0 + loop_radius + loop_radius * jnp.cos(theta)
    centre_y = 2.0 + loop_radius + loop_radius * jnp.sin(theta)
    spread = jax.random.uniform(keys[0], (2, count), jnp.float32, -1.25, 1.25)
    height = jax.random.uniform(keys[1], (1, count), jnp.float32, 0.0, 0.2)
    centres = jnp.concatenate([(centre_x + spread[0])[None, :], (centre_y + spread[1])[None, :], height], axis=0)
    along_y = jax.random.randint(keys[2], (count,), 0, 2).astype(jnp.float32)
    sign = 2.0 * jax.random.randint(keys[3], (count,), 0, 2).astype(jnp.float32) - 1.0
    tilt = 0.3 * jax.random.normal(keys[4], (3, count), jnp.float32)
    raw_dir = jnp.stack([sign * (1.0 - along_y) + tilt[0], sign * along_y + tilt[1], 0.3 * tilt[2]])
    direction = raw_dir / jnp.sqrt(jnp.sum(raw_dir * raw_dir, axis=0, keepdims=True))
    length = jnp.exp(jax.random.uniform(keys[5], (1, count), jnp.float32, jnp.log(0.2), jnp.log(2.0)))
    radius = jnp.exp(jax.random.uniform(keys[6], (1, count), jnp.float32, jnp.log(0.05), jnp.log(0.5)))
    return jnp.concatenate([centres, direction, length, radius], axis=0).astype(jnp.float32)


def draw_pair_on(key, part):
    base = jax.random.randint(jax.random.fold_in(key, 23), (N_BLK, REACH), 0, 4)
    marks = (base > 0).astype(jnp.int32)
    lower = [jnp.roll(marks[:, k], k + 1) for k in range(REACH)]
    upper = [marks[:, k] for k in range(REACH)]
    return jnp.stack(lower + upper, axis=1).astype(jnp.int32)


def plant(values, own_key, least, high):
    dims = values.shape
    place = [jax.random.randint(jax.random.fold_in(own_key, axis), (), 0, dims[axis]) for axis in range(len(dims))]
    values = values.at[tuple(place)].set(least)
    longest = dims.index(max(dims))
    place[longest] = (place[longest] + 1) % dims[longest]
    return values.at[tuple(place)].set(high)


def shard_levels(rng, dims, pieces, low, largest):
    factor_of = 1.0
    for dim, parts in pieces:
        heights = jax.random.uniform(jax.random.fold_in(jax.random.fold_in(rng, 6), dim), (parts,), jnp.float32, low / len(pieces), largest / len(pieces))
        factor_of = factor_of * jnp.repeat(jnp.exp(heights), dims[dim] // parts).reshape((-1,) + (1,) * (len(dims) - 1 - dim))
    return factor_of


def centred(stream_key, extent, scale, limit, shards=(), kind=jnp.bfloat16):
    level = shard_levels(stream_key, extent, shards, -0.22, 0.18) if shards else 1.0
    array = jax.random.normal(stream_key, extent, jnp.float32) * scale * level
    return jnp.minimum(jnp.maximum(array, -limit), limit).astype(kind)


def setup_inputs(seed: int = 0) -> dict:
    splits = jax.random.split(jax.random.key(seed), 5)
    geometry = draw_geometry(jax.random.fold_in(splits[4], 71), 0)
    currents = centred(splits[1], (COLS, SEGMENTS), 1.0, 6.0, ((1, 512),), jnp.float32)
    net_ids = plant(jax.random.randint(splits[2], (SEGMENTS,), 0, NETS), jax.random.fold_in(splits[2], 1), 0, NETS - 1).astype(jnp.int32)
    pair_on = draw_pair_on(jax.random.fold_in(splits[4], 71), 0)
    return dict(geometry=geometry, currents=currents, net_ids=net_ids, pair_on=pair_on)


def kernel_tile(own, other):
    delta_x = own[0][:, None] - other[0][None, :]
    delta_y = own[1][:, None] - other[1][None, :]
    delta_z = own[2][:, None] - other[2][None, :]
    dist_sq = delta_x * delta_x + delta_y * delta_y + delta_z * delta_z
    radius_sq = (own[7] * own[7])[:, None] + (other[7] * other[7])[None, :]
    cosine = own[3][:, None] * other[3][None, :] + own[4][:, None] * other[4][None, :] + own[5][:, None] * other[5][None, :]
    lengths = own[6][:, None] * other[6][None, :]
    netf = jnp.where(own[8][:, None] == other[8][None, :], jnp.float32(1.0), jnp.float32(0.5))
    return cosine * lengths * netf * 0.1 / jnp.sqrt(dist_sq + radius_sq)

def apply_tile(own, other):
    tile = kernel_tile(own, other)
    return lax.dot_general(other[9:], tile, (((1,), (1,)), ((), ())), precision=lax.Precision.HIGHEST, preferred_element_type=jnp.float32)

def reference(geometry, currents, net_ids, pair_on):
    packed = jnp.concatenate([geometry, net_ids.astype(jnp.float32)[None, :], currents], axis=0)
    rows_all = packed.shape[0]
    blocks = packed.reshape(rows_all, N_BLK, SEG_DEV).transpose(1, 0, 2)
    offsets = [-(k + 1) for k in range(REACH)] + [k + 1 for k in range(REACH)]

    def one_block(index):
        own = lax.dynamic_index_in_dim(blocks, index, 0, keepdims=False)
        total = apply_tile(own, own)
        for position, offset in enumerate(offsets):
            where = ((index + offset) % N_BLK).astype(jnp.int32)
            other = lax.dynamic_index_in_dim(blocks, where, 0, keepdims=False)
            flag = lax.dynamic_index_in_dim(pair_on[:, position], index, 0, keepdims=False).astype(jnp.float32)
            total = total + flag * apply_tile(own, other)
        return total
    result = lax.map(one_block, jnp.arange(N_BLK, dtype=jnp.int32))
    return result.transpose(1, 0, 2).reshape(COLS, SEGMENTS)
```

```python
import functools

import jax
import jax.numpy as jnp
from jax import lax
from jax.experimental import pallas as pl
from jax.experimental.pallas import tpu as pltpu
from jax.sharding import PartitionSpec as P

F32 = jnp.float32
BF16 = jnp.bfloat16
NETS = 4
GEO = 8
LANES = 128
ROWS = 256


def from_behind(block, axis, distance):
    devices = range(lax.axis_size(axis))
    route = [((i - distance) % len(devices), i) for i in devices]
    return lax.ppermute(block, axis, route)


def in_two(value):
    high = value.astype(BF16)
    return high, (value - high.astype(F32)).astype(BF16)


def in_three(value):
    high = value.astype(BF16)
    rest = value - high.astype(F32)
    middle = rest.astype(BF16)
    return high, middle, (rest - middle.astype(F32)).astype(BF16)


def by_net(geo, same, different):
    net = geo[7:8]
    rows = [geo[4:7] * jnp.where(net == F32(n), F32(same), F32(different)) for n in range(NETS)]
    pad = jnp.zeros((16 - 3 * NETS, geo.shape[1]), F32)
    return jnp.concatenate(rows + [pad], axis=0)


def own_factor(geo):
    high, middle, low = in_three(by_net(geo, 0.1, 0.05))
    return jnp.concatenate([high, high, middle, middle, high, low], axis=0)


def other_factor(geo):
    high, middle, low = in_three(by_net(geo, 1.0, 0.0))
    return jnp.concatenate([high, middle, high, middle, low, high], axis=0)


def tiles_kernel(plan, has_acc, last, *refs):
    n_blocks = 1 + max(operand for operand, _, _ in plan)
    flags, own = refs[:2]
    blocks = refs[2 : 2 + n_blocks]
    acc_in = refs[2 + n_blocks] if has_acc else None
    out = refs[2 + n_blocks + has_acc]
    cols, left, right, cur, total = refs[3 + n_blocks + has_acc :]
    seg = own.shape[1]

    geo = own[0:GEO]
    turned = jnp.transpose(geo)
    for q in range(4):
        cols[q] = jnp.broadcast_to(turned[:, q : q + 1], (seg, LANES))
    left[...] = jnp.transpose(own_factor(geo))
    acc = total if last else out
    if has_acc:
        acc[...] = acc_in[...]
    else:
        acc[...] = jnp.zeros_like(acc)

    for operand, first, position in plan:
        ref = blocks[operand]
        geo = ref[first : first + GEO]
        factor = geo
        if position is not None:
            factor = geo * flags[0, position].astype(F32)
            factor = jnp.concatenate([factor[0:7], geo[7:8]], axis=0)
        right[...] = other_factor(factor)
        cur[...] = jnp.concatenate(in_two(ref[first + GEO : first + GEO + 32]), axis=0)
        row_x, row_y = geo[0:1], geo[1:2]
        row_z, row_a = geo[2:3] * F32(-2.0), geo[3:4]

        def chunk(k, carry):
            at = pl.ds(pl.multiple_of(k * ROWS, ROWS), ROWS)
            wide = lambda q: jnp.tile(cols[q, at, :], (1, seg // LANES))
            moment = jnp.dot(left[at, :], right[...], preferred_element_type=F32)
            dx = wide(0) - row_x
            dy = wide(1) - row_y
            span = (wide(2) * row_z + (wide(3) + row_a)) + (dx * dx + dy * dy)
            high, low = in_two(moment * lax.rsqrt(span))
            nt = (((1,), (1,)), ((), ()))
            both = lax.dot_general(high, cur[...], nt, preferred_element_type=F32)
            rest = lax.dot_general(low, cur[0:32, :], nt, preferred_element_type=F32)
            acc[at, :] += both[:, 0:32] + both[:, 32:64] + rest
            return carry

        lax.fori_loop(0, seg // ROWS, chunk, 0, unroll=True)
    if last:
        out[...] = jnp.transpose(total[...])


def tiles(flags, own, blocks, plan, acc=None, last=False):
    seg = own.shape[1]
    vmem = pl.BlockSpec(memory_space=pltpu.VMEM)
    operands = [flags, own, *blocks] + ([] if acc is None else [acc])
    n = len(plan)
    return pl.pallas_call(
        functools.partial(tiles_kernel, plan, acc is not None, last),
        out_shape=jax.ShapeDtypeStruct((32, seg) if last else (seg, 32), F32),
        in_specs=[pl.BlockSpec(memory_space=pltpu.SMEM)] + [vmem] * (len(operands) - 1),
        out_specs=vmem,
        scratch_shapes=[
            pltpu.VMEM((4, seg, LANES), F32),
            pltpu.VMEM((seg, 96), BF16),
            pltpu.VMEM((96, seg), BF16),
            pltpu.VMEM((64, seg), BF16),
            pltpu.VMEM((seg, 32), F32),
        ],
        compiler_params=pltpu.CompilerParams(vmem_limit_bytes=40 << 20),
        cost_estimate=pl.CostEstimate(
            flops=n * 2 * seg * seg * 192, bytes_accessed=n * 40 * seg * 4, transcendentals=n * seg * seg
        ),
    )(*operands)


def shards(geometry, currents, net_ids, pair_on):
    z, radius = geometry[2:3], geometry[7:8]
    packed = jnp.concatenate(
        [
            geometry[0:3],
            z * z + radius * radius,
            geometry[3:6] * geometry[6:7],
            net_ids.astype(F32)[None, :],
            currents,
        ],
        axis=0,
    )
    rows = packed.shape[0]
    below1 = from_behind(packed, "blk", 1)
    below2 = from_behind(packed, "blk", 2)
    above1 = from_behind(packed, "blk", -1)
    above2 = from_behind(packed, "blk", -2)
    acc = tiles(pair_on, packed, [packed], [(0, 0, None)])
    far_below = from_behind(jnp.concatenate([below1, below2], axis=0), "blk", 2)
    far_above = from_behind(jnp.concatenate([above1, above2], axis=0), "blk", -2)
    near = [below1, below2, above1, above2]
    acc = tiles(pair_on, packed, near, [(0, 0, 0), (1, 0, 1), (2, 0, 4), (3, 0, 5)], acc)
    far = [far_below, far_above]
    return tiles(pair_on, packed, far, [(0, 0, 2), (0, rows, 3), (1, 0, 6), (1, rows, 7)], acc, last=True)


def solution(mesh):
    return jax.shard_map(
        shards,
        mesh=mesh,
        in_specs=(P(None, "blk"), P(None, "blk"), P("blk"), P("blk", None)),
        out_specs=P(None, "blk"),
        check_vma=False,
    )
```

```python
import functools

import jax
import jax.numpy as jnp
from jax import lax
from jax.experimental import pallas as pl
from jax.experimental.pallas import tpu as pltpu
from jax.sharding import PartitionSpec as P

F32 = jnp.float32
BF16 = jnp.bfloat16
NETS = 4
GEO = 8
COLS = 32
BLOCK = GEO + COLS
LANES = 128
ROWS = 512
VMEM = pl.BlockSpec(memory_space=pltpu.VMEM)
SMEM = pl.BlockSpec(memory_space=pltpu.SMEM)


def swap(block, pair_of):
    return lax.ppermute(block, "blk", [(i, pair_of(i)) for i in range(lax.axis_size("blk"))])


def in_two(value):
    high = value.astype(BF16)
    return high, (value - high.astype(F32)).astype(BF16)


def in_three(value):
    high = value.astype(BF16)
    rest = value - high.astype(F32)
    middle = rest.astype(BF16)
    return high, middle, (rest - middle.astype(F32)).astype(BF16)


def by_net(geo, moments, same, different):
    net = geo[7:8]
    rows = [moments * jnp.where(net == F32(n), F32(same), F32(different)) for n in range(NETS)]
    pad = jnp.zeros((16 - 3 * NETS, geo.shape[1]), F32)
    return jnp.concatenate(rows + [pad], axis=0)


def own_factor(geo):
    high, middle, low = in_three(by_net(geo, geo[4:7], 0.1, 0.05))
    return jnp.concatenate([high, high, middle, middle, high, low], axis=0)


def other_factor(geo, flag):
    moments = geo[4:7] if flag is None else geo[4:7] * flag
    high, middle, low = in_three(by_net(geo, moments, 1.0, 0.0))
    return jnp.concatenate([high, middle, high, middle, low, high], axis=0)


def pack_kernel(geometry, currents, nets, out):
    geo = geometry[...]
    z, radius = geo[2:3], geo[7:8]
    rows = [geo[0:3], z * z + radius * radius, geo[3:6] * geo[6:7], nets[...].astype(F32)]
    out[0:GEO] = jnp.concatenate(rows, axis=0)
    out[GEO:BLOCK] = currents[...]


def place():
    at = lax.axis_index("blk")
    return at & 1, (at >> 1) & 1, (at >> 2) & 1


def flag_at(flags, offset):
    return flags[0, jnp.where(offset < 0, -offset - 1, offset + 3)].astype(F32)


def add_tile(voltage, ref, first, flag, cols, left, right, cur):
    seg = left.shape[0]
    geo = ref[first : first + GEO]
    right[...] = other_factor(geo, flag)
    cur[...] = jnp.concatenate(in_two(ref[first + GEO : first + BLOCK]), axis=0)
    row_x, row_y = geo[0:1], geo[1:2]
    row_z, row_a = geo[2:3] * F32(-2.0), geo[3:4]

    def chunk(k, carry):
        at = pl.ds(pl.multiple_of(k * ROWS, ROWS), ROWS)
        wide = lambda q: jnp.tile(cols[q, at, :], (1, seg // LANES))
        moment = jnp.dot(left[at, :], right[...], preferred_element_type=F32)
        dx = wide(0) - row_x
        dy = wide(1) - row_y
        span = (wide(2) * row_z + (wide(3) + row_a)) + (dx * dx + dy * dy)
        high, low = in_two(moment * lax.rsqrt(span))
        nt = (((1,), (1,)), ((), ()))
        both = lax.dot_general(cur[...], high, nt, preferred_element_type=F32)
        rest = lax.dot_general(cur[0:COLS, :], low, nt, preferred_element_type=F32)
        voltage[:, at] += both[0:COLS] + both[COLS : 2 * COLS] + rest
        return carry

    lax.fori_loop(0, seg // ROWS, chunk, 0, unroll=True)


def spread(turned, cols):
    for q in range(4):
        cols[q] = jnp.broadcast_to(turned[:, q : q + 1], cols.shape[1:])


def own_kernel(own, voltage, turned, left, cols, right, cur):
    geo = own[0:GEO]
    turned[...] = jnp.transpose(geo)
    left[...] = jnp.transpose(own_factor(geo))
    spread(turned[...], cols)
    voltage[...] = jnp.zeros_like(voltage)
    add_tile(voltage, own, 0, None, cols, left, right, cur)


def others_kernel(offsets, flags, turned, left, before, *refs):
    blocks, (voltage, cols, right, cur) = refs[:-4], refs[-4:]
    spread(turned[...], cols)
    voltage[...] = before[...]
    found = [(ref, first) for ref in blocks for first in range(0, ref.shape[0], BLOCK)]
    for (ref, first), offset in zip(found, offsets, strict=True):
        add_tile(voltage, ref, first, flag_at(flags, offset(*place())), cols, left, right, cur)


def scratch(seg):
    return [
        pltpu.VMEM((4, seg, LANES), F32),
        pltpu.VMEM((96, seg), BF16),
        pltpu.VMEM((2 * COLS, seg), BF16),
    ]


def params(n, seg):
    return dict(
        compiler_params=pltpu.CompilerParams(vmem_limit_bytes=40 << 20),
        cost_estimate=pl.CostEstimate(
            flops=n * 6 * seg * seg * 192, bytes_accessed=n * BLOCK * seg * 4, transcendentals=n * seg * seg
        ),
    )


def own_tile(own):
    seg = own.shape[1]
    return pl.pallas_call(
        own_kernel,
        out_shape=(
            jax.ShapeDtypeStruct((COLS, seg), F32),
            jax.ShapeDtypeStruct((seg, GEO), F32),
            jax.ShapeDtypeStruct((seg, 96), BF16),
        ),
        in_specs=[VMEM],
        out_specs=(VMEM, VMEM, VMEM),
        scratch_shapes=scratch(seg),
        **params(1, seg),
    )(own)


def other_tiles(flags, turned, left, voltage, blocks, offsets):
    seg = left.shape[0]
    return pl.pallas_call(
        functools.partial(others_kernel, offsets),
        out_shape=jax.ShapeDtypeStruct((COLS, seg), F32),
        in_specs=[SMEM] + [VMEM] * (3 + len(blocks)),
        out_specs=VMEM,
        scratch_shapes=scratch(seg),
        **params(len(offsets), seg),
    )(flags, turned, left, voltage, *blocks)


def sign(bit):
    return 1 - 2 * bit


def shards(geometry, currents, net_ids, pair_on):
    seg = geometry.shape[1]
    packed = pl.pallas_call(
        pack_kernel,
        out_shape=jax.ShapeDtypeStruct((BLOCK, seg), F32),
        in_specs=[VMEM] * 3,
        out_specs=VMEM,
    )(geometry, currents, net_ids[None, :])
    n = lax.axis_size("blk")
    core, chip, half = place()
    within = swap(packed, lambda i: i ^ 4)
    across = swap(packed, lambda i: (((i - 4) % n ^ 4) + 4) % n)
    voltage, turned, left = own_tile(packed)
    within, across, voltage = lax.optimization_barrier((within, across, voltage))
    fourth = jnp.where(chip != half, across, within)
    second = swap(jnp.concatenate([packed, fourth], axis=0), lambda i: i ^ 2)
    voltage = other_tiles(
        pair_on,
        turned,
        left,
        voltage,
        [within, across],
        [lambda core, chip, half: 4 * sign(half), lambda core, chip, half: -4 * sign(half)],
    )
    second, voltage = lax.optimization_barrier((second, voltage))
    fourth = jnp.where(core != half, across, within)
    first = swap(jnp.concatenate([packed, fourth, second], axis=0), lambda i: i ^ 1)
    voltage = other_tiles(
        pair_on,
        turned,
        left,
        voltage,
        [second],
        [lambda core, chip, half: 2 * sign(chip), lambda core, chip, half: -2 * sign(chip)],
    )
    return other_tiles(
        pair_on,
        turned,
        left,
        voltage,
        [first],
        [
            lambda core, chip, half: sign(core),
            lambda core, chip, half: -3 * sign(core),
            lambda core, chip, half: sign(core) + 2 * sign(chip),
            lambda core, chip, half: sign(core) - 2 * sign(chip),
        ],
    )


def solution(mesh):
    return jax.shard_map(
        shards,
        mesh=mesh,
        in_specs=(P(None, "blk"), P(None, "blk"), P("blk"), P("blk", None)),
        out_specs=P(None, "blk"),
        check_vma=False,
    )
```

```python
import functools

import jax
import jax.numpy as jnp
from jax import lax
from jax.experimental import pallas as pl
from jax.experimental.pallas import tpu as pltpu
from jax.sharding import PartitionSpec as P

F32 = jnp.float32
BF16 = jnp.bfloat16
NETS = 4
GEO = 8
COLS = 32
BLOCK = GEO + COLS
LANES = 128
ROWS = 256
VMEM = pl.BlockSpec(memory_space=pltpu.VMEM)


def swap(block, pair_of):
    return lax.ppermute(block, "blk", [(i, pair_of(i)) for i in range(lax.axis_size("blk"))])


def in_two(value):
    high = value.astype(BF16)
    return high, (value - high.astype(F32)).astype(BF16)


def in_three(value):
    high = value.astype(BF16)
    rest = value - high.astype(F32)
    middle = rest.astype(BF16)
    return high, middle, (rest - middle.astype(F32)).astype(BF16)


def by_net(geo, moments, same, different):
    net = geo[7:8]
    rows = [moments * jnp.where(net == F32(n), F32(same), F32(different)) for n in range(NETS)]
    pad = jnp.zeros((16 - 3 * NETS, geo.shape[1]), F32)
    return jnp.concatenate(rows + [pad], axis=0)


def own_factor(geo):
    high, middle, low = in_three(by_net(geo, geo[4:7], 0.1, 0.05))
    return jnp.concatenate([high, high, middle, middle, high, low], axis=0)


def other_factor(geo, flag):
    moments = geo[4:7] if flag is None else geo[4:7] * flag
    high, middle, low = in_three(by_net(geo, moments, 1.0, 0.0))
    return jnp.concatenate([high, middle, high, middle, low, high], axis=0)


def pack(geometry, currents, nets, out):
    geo = geometry[...]
    z, radius = geo[2:3], geo[7:8]
    rows = [geo[0:3], z * z + radius * radius, geo[3:6] * geo[6:7], nets[...].astype(F32)]
    out[0:GEO] = jnp.concatenate(rows, axis=0)
    out[GEO:BLOCK] = currents[...]


def pack_kernel(geometry, currents, nets, pairs, out, flags):
    pack(geometry, currents, nets, out)
    flags[...] = jnp.transpose(jnp.broadcast_to(pairs[...], (LANES, pairs.shape[1])).astype(F32))


def place():
    at = lax.axis_index("blk")
    return at & 1, (at >> 1) & 1, (at >> 2) & 1


def flag_at(flags, offset):
    return flags[pl.ds(jnp.where(offset < 0, -offset - 1, offset + 3), 1), 0:1]


def add_tiles(voltage, blocks, cols, left, right, cur, moment, high, low):
    seg = left.shape[0]
    chunks = seg // ROWS
    steps = len(blocks) * chunks
    nt = (((1,), (1,)), ((), ()))

    def moments(step):
        block, chunk = divmod(step, chunks)
        ref, first, flag = blocks[block]
        if chunk == 0:
            right[block % 2] = other_factor(ref[first : first + GEO], flag)
            cur[block % 2] = jnp.concatenate(in_two(ref[first + GEO : first + BLOCK]), axis=0)
        rows = left[chunk * ROWS : (chunk + 1) * ROWS, :]
        moment[step % 2] = jnp.dot(rows, right[block % 2], preferred_element_type=F32)

    def kernel(step):
        block, chunk = divmod(step, chunks)
        ref, first, _ = blocks[block]
        at = slice(chunk * ROWS, (chunk + 1) * ROWS)
        wide = lambda q: jnp.tile(cols[q, at, :], (1, seg // LANES))
        row = lambda q: ref[first + q : first + q + 1]
        dx = wide(0) - row(0)
        dy = wide(1) - row(1)
        span = (wide(2) * (row(2) * F32(-2.0)) + (wide(3) + row(3))) + (dx * dx + dy * dy)
        high[step % 2], low[step % 2] = in_two(moment[step % 2] * lax.rsqrt(span))

    def induce(step):
        block, chunk = divmod(step, chunks)
        at = slice(chunk * ROWS, (chunk + 1) * ROWS)
        both = lax.dot_general(cur[block % 2], high[step % 2], nt, preferred_element_type=F32)
        rest = lax.dot_general(cur[block % 2, 0:COLS], low[step % 2], nt, preferred_element_type=F32)
        voltage[:, at] += both[0:COLS] + both[COLS : 2 * COLS] + rest

    for step in range(steps + 2):
        if step >= 2:
            induce(step - 2)
        if step < steps:
            moments(step)
        if 1 <= step <= steps:
            kernel(step - 1)


def spread(turned, cols):
    for q in range(4):
        cols[q] = jnp.broadcast_to(turned[:, q : q + 1], cols.shape[1:])


def own_kernel(geometry, currents, nets, voltage, turned, left, own, cols, *buffers):
    pack(geometry, currents, nets, own)
    geo = own[0:GEO]
    turned[...] = jnp.transpose(geo)
    left[...] = jnp.transpose(own_factor(geo))
    spread(turned[...], cols)
    voltage[...] = jnp.zeros_like(voltage)
    add_tiles(voltage, [(own, 0, None)], cols, left, *buffers)


def others_kernel(offsets, n_refs, flags, turned, left, before, *refs):
    found = [(ref, first) for ref in refs[:n_refs] for first in range(0, ref.shape[0], BLOCK)]
    voltage, cols, *buffers = refs[n_refs:]
    spread(turned[...], cols)
    voltage[...] = before[...]
    blocks = [
        (ref, first, flag_at(flags, offset(*place()))) for (ref, first), offset in zip(found, offsets, strict=True)
    ]
    add_tiles(voltage, blocks, cols, left, *buffers)


def scratch(seg):
    return [
        pltpu.VMEM((4, seg, LANES), F32),
        pltpu.VMEM((2, 96, seg), BF16),
        pltpu.VMEM((2, 2 * COLS, seg), BF16),
        pltpu.VMEM((2, ROWS, seg), F32),
        pltpu.VMEM((2, ROWS, seg), BF16),
        pltpu.VMEM((2, ROWS, seg), BF16),
    ]


def params(n, seg):
    return dict(
        compiler_params=pltpu.CompilerParams(vmem_limit_bytes=40 << 20),
        cost_estimate=pl.CostEstimate(
            flops=n * 6 * seg * seg * 192, bytes_accessed=n * BLOCK * seg * 4, transcendentals=n * seg * seg
        ),
    )


def own_tile(geometry, currents, nets):
    seg = geometry.shape[1]
    return pl.pallas_call(
        own_kernel,
        out_shape=(
            jax.ShapeDtypeStruct((COLS, seg), F32),
            jax.ShapeDtypeStruct((seg, GEO), F32),
            jax.ShapeDtypeStruct((seg, 96), BF16),
            jax.ShapeDtypeStruct((BLOCK, seg), F32),
        ),
        in_specs=[VMEM] * 3,
        out_specs=(VMEM,) * 4,
        scratch_shapes=scratch(seg),
        **params(1, seg),
    )(geometry, currents, nets)


def other_tiles(flags, turned, left, voltage, blocks, offsets):
    seg = left.shape[0]
    return pl.pallas_call(
        functools.partial(others_kernel, offsets, len(blocks)),
        out_shape=jax.ShapeDtypeStruct((COLS, seg), F32),
        in_specs=[VMEM] * (4 + len(blocks)),
        out_specs=VMEM,
        scratch_shapes=scratch(seg),
        **params(len(offsets), seg),
    )(flags, turned, left, voltage, *blocks)


def sign(bit):
    return 1 - 2 * bit


def shards(geometry, currents, net_ids, pair_on):
    seg = geometry.shape[1]
    nets = net_ids[None, :]
    packed, flags = pl.pallas_call(
        pack_kernel,
        out_shape=(
            jax.ShapeDtypeStruct((BLOCK, seg), F32),
            jax.ShapeDtypeStruct((pair_on.shape[1], LANES), F32),
        ),
        in_specs=[VMEM] * 4,
        out_specs=(VMEM, VMEM),
    )(geometry, currents, nets, pair_on)
    n = lax.axis_size("blk")
    core, chip, half = place()
    within = swap(packed, lambda i: i ^ 4)
    across = swap(packed, lambda i: (((i - 4) % n ^ 4) + 4) % n)
    voltage, turned, left, own = own_tile(geometry, currents, nets)
    within, across, voltage = lax.optimization_barrier((within, across, voltage))
    fourth = jnp.where(chip != half, across, within)
    second = swap(jnp.concatenate([own, fourth], axis=0), lambda i: i ^ 2)
    voltage = other_tiles(
        flags,
        turned,
        left,
        voltage,
        [within, across],
        [lambda core, chip, half: 4 * sign(half), lambda core, chip, half: -4 * sign(half)],
    )
    second, voltage = lax.optimization_barrier((second, voltage))
    fourth = jnp.where(core != half, across, within)
    first = swap(jnp.concatenate([own, fourth, second], axis=0), lambda i: i ^ 1)
    voltage = other_tiles(
        flags,
        turned,
        left,
        voltage,
        [second],
        [lambda core, chip, half: 2 * sign(chip), lambda core, chip, half: -2 * sign(chip)],
    )
    return other_tiles(
        flags,
        turned,
        left,
        voltage,
        [first],
        [
            lambda core, chip, half: sign(core),
            lambda core, chip, half: -3 * sign(core),
            lambda core, chip, half: sign(core) + 2 * sign(chip),
            lambda core, chip, half: sign(core) - 2 * sign(chip),
        ],
    )


def solution(mesh):
    return jax.shard_map(
        shards,
        mesh=mesh,
        in_specs=(P(None, "blk"), P(None, "blk"), P("blk"), P("blk", None)),
        out_specs=P(None, "blk"),
        check_vma=False,
    )
```

```python
import functools

import jax
import jax.numpy as jnp
from jax import lax
from jax.experimental import pallas as pl
from jax.experimental.pallas import tpu as pltpu
from jax.sharding import PartitionSpec as P

F32 = jnp.float32
BF16 = jnp.bfloat16
NETS = 4
GEO = 8
COLS = 32
BLOCK = GEO + COLS
LANES = 128
ROWS = 256
VMEM = pl.BlockSpec(memory_space=pltpu.VMEM)


def swap(block, pair_of):
    return lax.ppermute(block, "blk", [(i, pair_of(i)) for i in range(lax.axis_size("blk"))])


def in_two(value):
    high = value.astype(BF16)
    return high, (value - high.astype(F32)).astype(BF16)


def in_three(value):
    high = value.astype(BF16)
    rest = value - high.astype(F32)
    middle = rest.astype(BF16)
    return high, middle, (rest - middle.astype(F32)).astype(BF16)


def by_net(geo, moments, same, different):
    net = geo[7:8]
    rows = [moments * jnp.where(net == F32(n), F32(same), F32(different)) for n in range(NETS)]
    pad = jnp.zeros((16 - 3 * NETS, geo.shape[1]), F32)
    return jnp.concatenate(rows + [pad], axis=0)


def own_factor(geo):
    high, middle, low = in_three(by_net(geo, geo[4:7], 0.1, 0.05))
    return jnp.concatenate([high, high, middle, middle, high, low], axis=0)


def other_factor(geo, flag):
    moments = geo[4:7] if flag is None else geo[4:7] * flag
    high, middle, low = in_three(by_net(geo, moments, 1.0, 0.0))
    return jnp.concatenate([high, middle, high, middle, low, high], axis=0)


def pack(geometry, currents, nets, out):
    geo = geometry[...]
    z, radius = geo[2:3], geo[7:8]
    rows = [geo[0:3], z * z + radius * radius, geo[3:6] * geo[6:7], nets[...].astype(F32)]
    out[0:GEO] = jnp.concatenate(rows, axis=0)
    out[GEO:BLOCK] = currents[...]


def pack_kernel(geometry, currents, nets, pairs, out, flags):
    pack(geometry, currents, nets, out)
    flags[...] = jnp.transpose(jnp.broadcast_to(pairs[...], (LANES, pairs.shape[1])).astype(F32))


def place():
    at = lax.axis_index("blk")
    return at & 1, (at >> 1) & 1, (at >> 2) & 1


def flag_at(flags, offset):
    return flags[pl.ds(jnp.where(offset < 0, -offset - 1, offset + 3), 1), 0:1]


def add_tiles(voltage, blocks, cols, left, right, cur, moment, high, low):
    seg = left.shape[0]
    chunks = seg // ROWS
    steps = len(blocks) * chunks
    nt = (((1,), (1,)), ((), ()))

    def moments(step):
        block, chunk = divmod(step, chunks)
        ref, first, flag = blocks[block]
        if chunk == 0:
            right[block % 2] = other_factor(ref[first : first + GEO], flag)
            cur[block % 2] = jnp.concatenate(in_two(ref[first + GEO : first + BLOCK]), axis=0)
        rows = left[chunk * ROWS : (chunk + 1) * ROWS, :]
        moment[step % 2] = jnp.dot(rows, right[block % 2], preferred_element_type=F32)

    def kernel(step):
        block, chunk = divmod(step, chunks)
        ref, first, _ = blocks[block]
        at = slice(chunk * ROWS, (chunk + 1) * ROWS)
        wide = lambda q: jnp.tile(cols[q, at, :], (1, seg // LANES))
        row = lambda q: ref[first + q : first + q + 1]
        dx = wide(0) - row(0)
        dy = wide(1) - row(1)
        span = (wide(2) * (row(2) * F32(-2.0)) + (wide(3) + row(3))) + (dx * dx + dy * dy)
        high[step % 2], low[step % 2] = in_two(moment[step % 2] * lax.rsqrt(span))

    def induce(step):
        block, chunk = divmod(step, chunks)
        at = slice(chunk * ROWS, (chunk + 1) * ROWS)
        both = lax.dot_general(cur[block % 2], high[step % 2], nt, preferred_element_type=F32)
        rest = lax.dot_general(cur[block % 2, 0:COLS], low[step % 2], nt, preferred_element_type=F32)
        voltage[:, at] += both[0:COLS] + both[COLS : 2 * COLS] + rest

    for step in range(steps + 2):
        if step >= 2:
            induce(step - 2)
        if step < steps:
            moments(step)
        if 1 <= step <= steps:
            kernel(step - 1)


def spread(turned, cols):
    for q in range(4):
        cols[q] = jnp.broadcast_to(turned[:, q : q + 1], cols.shape[1:])


def own_kernel(own, voltage, turned, left, cols, *buffers):
    geo = own[0:GEO]
    turned[...] = jnp.transpose(geo)
    left[...] = jnp.transpose(own_factor(geo))
    spread(turned[...], cols)
    voltage[...] = jnp.zeros_like(voltage)
    add_tiles(voltage, [(own, 0, None)], cols, left, *buffers)


def others_kernel(offsets, n_refs, flags, turned, left, before, *refs):
    found = [(ref, first) for ref in refs[:n_refs] for first in range(0, ref.shape[0], BLOCK)]
    voltage, cols, *buffers = refs[n_refs:]
    spread(turned[...], cols)
    voltage[...] = before[...]
    blocks = [
        (ref, first, flag_at(flags, offset(*place()))) for (ref, first), offset in zip(found, offsets, strict=True)
    ]
    add_tiles(voltage, blocks, cols, left, *buffers)


def scratch(seg):
    return [
        pltpu.VMEM((4, seg, LANES), F32),
        pltpu.VMEM((2, 96, seg), BF16),
        pltpu.VMEM((2, 2 * COLS, seg), BF16),
        pltpu.VMEM((2, ROWS, seg), F32),
        pltpu.VMEM((2, ROWS, seg), BF16),
        pltpu.VMEM((2, ROWS, seg), BF16),
    ]


def params(n, seg):
    return dict(
        compiler_params=pltpu.CompilerParams(vmem_limit_bytes=40 << 20),
        cost_estimate=pl.CostEstimate(
            flops=n * 6 * seg * seg * 192, bytes_accessed=n * BLOCK * seg * 4, transcendentals=n * seg * seg
        ),
    )


def own_tile(own):
    seg = own.shape[1]
    return pl.pallas_call(
        own_kernel,
        out_shape=(
            jax.ShapeDtypeStruct((COLS, seg), F32),
            jax.ShapeDtypeStruct((seg, GEO), F32),
            jax.ShapeDtypeStruct((seg, 96), BF16),
        ),
        in_specs=[VMEM],
        out_specs=(VMEM,) * 3,
        scratch_shapes=scratch(seg),
        **params(1, seg),
    )(own)


def other_tiles(flags, turned, left, voltage, blocks, offsets):
    seg = left.shape[0]
    return pl.pallas_call(
        functools.partial(others_kernel, offsets, len(blocks)),
        out_shape=jax.ShapeDtypeStruct((COLS, seg), F32),
        in_specs=[VMEM] * (4 + len(blocks)),
        out_specs=VMEM,
        scratch_shapes=scratch(seg),
        **params(len(offsets), seg),
    )(flags, turned, left, voltage, *blocks)


def sign(bit):
    return 1 - 2 * bit


def shards(geometry, currents, net_ids, pair_on):
    seg = geometry.shape[1]
    nets = net_ids[None, :]
    packed, flags = pl.pallas_call(
        pack_kernel,
        out_shape=(
            pltpu.VMEM((BLOCK, seg), F32),
            pltpu.VMEM((pair_on.shape[1], LANES), F32),
        ),
        in_specs=[VMEM] * 4,
        out_specs=(VMEM, VMEM),
    )(geometry, currents, nets, pair_on)
    n = lax.axis_size("blk")
    core, chip, half = place()
    within = swap(packed, lambda i: i ^ 4)
    across = swap(packed, lambda i: (((i - 4) % n ^ 4) + 4) % n)
    voltage, turned, left = own_tile(packed)
    across, within, voltage = lax.optimization_barrier((across, within, voltage))
    fourth = jnp.where(chip != half, across, within)
    second = swap(jnp.concatenate([packed, fourth], axis=0), lambda i: i ^ 2)
    voltage = other_tiles(
        flags,
        turned,
        left,
        voltage,
        [across, within],
        [lambda core, chip, half: -4 * sign(half), lambda core, chip, half: 4 * sign(half)],
    )
    second, voltage = lax.optimization_barrier((second, voltage))
    fourth = jnp.where(core != half, across, within)
    first = swap(jnp.concatenate([packed, fourth, second], axis=0), lambda i: i ^ 1)
    voltage = other_tiles(
        flags,
        turned,
        left,
        voltage,
        [second],
        [lambda core, chip, half: 2 * sign(chip), lambda core, chip, half: -2 * sign(chip)],
    )
    return other_tiles(
        flags,
        turned,
        left,
        voltage,
        [first],
        [
            lambda core, chip, half: sign(core),
            lambda core, chip, half: -3 * sign(core),
            lambda core, chip, half: sign(core) + 2 * sign(chip),
            lambda core, chip, half: sign(core) - 2 * sign(chip),
        ],
    )


def solution(mesh):
    return jax.shard_map(
        shards,
        mesh=mesh,
        in_specs=(P(None, "blk"), P(None, "blk"), P("blk"), P("blk", None)),
        out_specs=P(None, "blk"),
        check_vma=False,
    )
```

```python
import functools

import jax
import jax.numpy as jnp
from jax import lax
from jax.experimental import pallas as pl
from jax.experimental.pallas import tpu as pltpu
from jax.sharding import PartitionSpec as P

F32 = jnp.float32
BF16 = jnp.bfloat16
NETS = 4
GEO = 8
COLS = 32
BLOCK = GEO + COLS
LANES = 128
ROWS = 256
VMEM = pl.BlockSpec(memory_space=pltpu.VMEM)


def swap(block, pair_of):
    return lax.ppermute(block, "blk", [(i, pair_of(i)) for i in range(lax.axis_size("blk"))])


def in_two(value):
    high = value.astype(BF16)
    return high, (value - high.astype(F32)).astype(BF16)


def in_three(value):
    high = value.astype(BF16)
    rest = value - high.astype(F32)
    middle = rest.astype(BF16)
    return high, middle, (rest - middle.astype(F32)).astype(BF16)


def by_net(geo, moments, same, different):
    net = geo[7:8]
    rows = [moments * jnp.where(net == F32(n), F32(same), F32(different)) for n in range(NETS)]
    pad = jnp.zeros((16 - 3 * NETS, geo.shape[1]), F32)
    return jnp.concatenate(rows + [pad], axis=0)


def own_factor(geo):
    high, middle, low = in_three(by_net(geo, geo[4:7], 0.1, 0.05))
    return jnp.concatenate([high, high, middle, middle, high, low], axis=0)


def other_factor(geo, flag):
    moments = geo[4:7] if flag is None else geo[4:7] * flag
    high, middle, low = in_three(by_net(geo, moments, 1.0, 0.0))
    return jnp.concatenate([high, middle, high, middle, low, high], axis=0)


def pack(geometry, currents, nets, out):
    geo = geometry[...]
    z, radius = geo[2:3], geo[7:8]
    rows = [geo[0:3], z * z + radius * radius, geo[3:6] * geo[6:7], nets[...].astype(F32)]
    out[0:GEO] = jnp.concatenate(rows, axis=0)
    out[GEO:BLOCK] = currents[...]


def pack_kernel(geometry, currents, nets, pairs, out, flags):
    pack(geometry, currents, nets, out)
    flags[...] = jnp.transpose(jnp.broadcast_to(pairs[...], (LANES, pairs.shape[1])).astype(F32))


def place():
    at = lax.axis_index("blk")
    return at & 1, (at >> 1) & 1, (at >> 2) & 1


def flag_at(flags, offset):
    return flags[pl.ds(jnp.where(offset < 0, -offset - 1, offset + 3), 1), 0:1]


def add_tiles(voltage, blocks, cols, left, right, cur, moment, high, low):
    seg = left.shape[0]
    nt = (((1,), (1,)), ((), ()))
    spans = [(block, first, ROWS) for block in range(len(blocks)) for first in range(0, seg, ROWS)]
    block, first, size = spans.pop()
    spans += [(block, first, size // 2), (block, first + size // 2, size // 2)]
    steps = len(spans)

    def moments(step):
        block, start, size = spans[step]
        ref, first, flag = blocks[block]
        if start == 0:
            right[block % 2] = other_factor(ref[first : first + GEO], flag)
            cur[block % 2] = jnp.concatenate(in_two(ref[first + GEO : first + BLOCK]), axis=0)
        rows = left[start : start + size, :]
        moment[step % 2, 0:size] = jnp.dot(rows, right[block % 2], preferred_element_type=F32)

    def kernel(step):
        block, start, size = spans[step]
        ref, first, _ = blocks[block]
        wide = lambda q: jnp.tile(cols[q, start : start + size, :], (1, seg // LANES))
        row = lambda q: ref[first + q : first + q + 1]
        dx = wide(0) - row(0)
        dy = wide(1) - row(1)
        span = (wide(2) * (row(2) * F32(-2.0)) + (wide(3) + row(3))) + (dx * dx + dy * dy)
        both = in_two(moment[step % 2, 0:size] * lax.rsqrt(span))
        high[step % 2, 0:size], low[step % 2, 0:size] = both

    def induce(step):
        block, start, size = spans[step]
        at = slice(start, start + size)
        both = lax.dot_general(cur[block % 2], high[step % 2, 0:size], nt, preferred_element_type=F32)
        rest = lax.dot_general(cur[block % 2, 0:COLS], low[step % 2, 0:size], nt, preferred_element_type=F32)
        voltage[:, at] += both[0:COLS] + both[COLS : 2 * COLS] + rest

    for step in range(steps + 2):
        if step >= 2:
            induce(step - 2)
        if step < steps:
            moments(step)
        if 1 <= step <= steps:
            kernel(step - 1)


def spread(turned, cols):
    for q in range(4):
        cols[q] = jnp.broadcast_to(turned[:, q : q + 1], cols.shape[1:])


def own_kernel(own, voltage, turned, left, cols, *buffers):
    geo = own[0:GEO]
    turned[...] = jnp.transpose(geo)
    left[...] = jnp.transpose(own_factor(geo))
    spread(turned[...], cols)
    voltage[...] = jnp.zeros_like(voltage)
    add_tiles(voltage, [(own, 0, None)], cols, left, *buffers)


def others_kernel(offsets, n_refs, flags, turned, left, before, *refs):
    found = [(ref, first) for ref in refs[:n_refs] for first in range(0, ref.shape[0], BLOCK)]
    voltage, cols, *buffers = refs[n_refs:]
    spread(turned[...], cols)
    voltage[...] = before[...]
    blocks = [
        (ref, first, flag_at(flags, offset(*place()))) for (ref, first), offset in zip(found, offsets, strict=True)
    ]
    add_tiles(voltage, blocks, cols, left, *buffers)


def scratch(seg):
    return [
        pltpu.VMEM((4, seg, LANES), F32),
        pltpu.VMEM((2, 96, seg), BF16),
        pltpu.VMEM((2, 2 * COLS, seg), BF16),
        pltpu.VMEM((2, ROWS, seg), F32),
        pltpu.VMEM((2, ROWS, seg), BF16),
        pltpu.VMEM((2, ROWS, seg), BF16),
    ]


def params(n, seg):
    return dict(
        compiler_params=pltpu.CompilerParams(vmem_limit_bytes=40 << 20),
        cost_estimate=pl.CostEstimate(
            flops=n * 6 * seg * seg * 192, bytes_accessed=n * BLOCK * seg * 4, transcendentals=n * seg * seg
        ),
    )


def own_tile(own):
    seg = own.shape[1]
    return pl.pallas_call(
        own_kernel,
        out_shape=(
            jax.ShapeDtypeStruct((COLS, seg), F32),
            jax.ShapeDtypeStruct((seg, GEO), F32),
            jax.ShapeDtypeStruct((seg, 96), BF16),
        ),
        in_specs=[VMEM],
        out_specs=(VMEM,) * 3,
        scratch_shapes=scratch(seg),
        **params(1, seg),
    )(own)


def other_tiles(flags, turned, left, voltage, blocks, offsets):
    seg = left.shape[0]
    return pl.pallas_call(
        functools.partial(others_kernel, offsets, len(blocks)),
        out_shape=jax.ShapeDtypeStruct((COLS, seg), F32),
        in_specs=[VMEM] * (4 + len(blocks)),
        out_specs=VMEM,
        scratch_shapes=scratch(seg),
        **params(len(offsets), seg),
    )(flags, turned, left, voltage, *blocks)


def sign(bit):
    return 1 - 2 * bit


def shards(geometry, currents, net_ids, pair_on):
    seg = geometry.shape[1]
    nets = net_ids[None, :]
    packed, flags = pl.pallas_call(
        pack_kernel,
        out_shape=(
            pltpu.VMEM((BLOCK, seg), F32),
            pltpu.VMEM((pair_on.shape[1], LANES), F32),
        ),
        in_specs=[VMEM] * 4,
        out_specs=(VMEM, VMEM),
    )(geometry, currents, nets, pair_on)
    n = lax.axis_size("blk")
    core, chip, half = place()
    within = swap(packed, lambda i: i ^ 4)
    across = swap(packed, lambda i: (((i - 4) % n ^ 4) + 4) % n)
    voltage, turned, left = own_tile(packed)
    across, within, voltage = lax.optimization_barrier((across, within, voltage))
    fourth = jnp.where(chip != half, across, within)
    second = swap(jnp.concatenate([packed, fourth], axis=0), lambda i: i ^ 2)
    voltage = other_tiles(
        flags,
        turned,
        left,
        voltage,
        [across, within],
        [lambda core, chip, half: -4 * sign(half), lambda core, chip, half: 4 * sign(half)],
    )
    second, voltage = lax.optimization_barrier((second, voltage))
    fourth = jnp.where(core != half, across, within)
    first = swap(jnp.concatenate([packed, fourth, second], axis=0), lambda i: i ^ 1)
    voltage = other_tiles(
        flags,
        turned,
        left,
        voltage,
        [second],
        [lambda core, chip, half: 2 * sign(chip), lambda core, chip, half: -2 * sign(chip)],
    )
    return other_tiles(
        flags,
        turned,
        left,
        voltage,
        [first],
        [
            lambda core, chip, half: sign(core),
            lambda core, chip, half: -3 * sign(core),
            lambda core, chip, half: sign(core) + 2 * sign(chip),
            lambda core, chip, half: sign(core) - 2 * sign(chip),
        ],
    )


def solution(mesh):
    return jax.shard_map(
        shards,
        mesh=mesh,
        in_specs=(P(None, "blk"), P(None, "blk"), P("blk"), P("blk", None)),
        out_specs=P(None, "blk"),
        check_vma=False,
    )
```

```python
import functools

import jax
import jax.numpy as jnp
from jax import lax
from jax.experimental import pallas as pl
from jax.experimental.pallas import tpu as pltpu
from jax.sharding import PartitionSpec as P

F32 = jnp.float32
BF16 = jnp.bfloat16
NETS = 4
GEO = 8
COLS = 32
BLOCK = GEO + COLS
LANES = 128
ROWS = 256
VMEM = pl.BlockSpec(memory_space=pltpu.VMEM)


def swap(block, pair_of):
    return lax.ppermute(block, "blk", [(i, pair_of(i)) for i in range(lax.axis_size("blk"))])


def in_two(value):
    high = value.astype(BF16)
    return high, (value - high.astype(F32)).astype(BF16)


def in_three(value):
    high = value.astype(BF16)
    rest = value - high.astype(F32)
    middle = rest.astype(BF16)
    return high, middle, (rest - middle.astype(F32)).astype(BF16)


def by_net(geo, moments, same, different):
    net = geo[7:8]
    rows = [moments * jnp.where(net == F32(n), F32(same), F32(different)) for n in range(NETS)]
    pad = jnp.zeros((16 - 3 * NETS, geo.shape[1]), F32)
    return jnp.concatenate(rows + [pad], axis=0)


def own_factor(geo):
    high, middle, low = in_three(by_net(geo, geo[4:7], 0.1, 0.05))
    return jnp.concatenate([high, high, middle, middle, high, low], axis=0)


def other_factor(geo, flag):
    moments = geo[4:7] if flag is None else geo[4:7] * flag
    high, middle, low = in_three(by_net(geo, moments, 1.0, 0.0))
    return jnp.concatenate([high, middle, high, middle, low, high], axis=0)


def pack(geometry, currents, nets, out):
    geo = geometry[...]
    z, radius = geo[2:3], geo[7:8]
    rows = [geo[0:3], z * z + radius * radius, geo[3:6] * geo[6:7], nets[...].astype(F32)]
    out[0:GEO] = jnp.concatenate(rows, axis=0)
    out[GEO:BLOCK] = currents[...]


def pack_kernel(geometry, currents, nets, pairs, out, flags):
    pack(geometry, currents, nets, out)
    flags[...] = jnp.transpose(jnp.broadcast_to(pairs[...], (LANES, pairs.shape[1])).astype(F32))


def place():
    at = lax.axis_index("blk")
    return at & 1, (at >> 1) & 1, (at >> 2) & 1


def flag_at(flags, offset):
    return flags[pl.ds(jnp.where(offset < 0, -offset - 1, offset + 3), 1), 0:1]


def add_tiles(voltage, blocks, cols, left, right, cur, moment, high, low):
    seg = left.shape[0]
    nt = (((1,), (1,)), ((), ()))
    spans = [(block, first, ROWS) for block in range(len(blocks)) for first in range(0, seg, ROWS)]
    block, first, size = spans.pop()
    spans += [(block, first, size // 2), (block, first + size // 2, size // 2)]
    block, first, size = spans.pop(0)
    spans = [(block, first, size // 2), (block, first + size // 2, size // 2)] + spans
    steps = len(spans)

    def moments(step):
        block, start, size = spans[step]
        ref, first, flag = blocks[block]
        if start == 0:
            right[block % 2] = other_factor(ref[first : first + GEO], flag)
            cur[block % 2] = jnp.concatenate(in_two(ref[first + GEO : first + BLOCK]), axis=0)
        rows = left[start : start + size, :]
        moment[step % 2, 0:size] = jnp.dot(rows, right[block % 2], preferred_element_type=F32)

    def kernel(step):
        block, start, size = spans[step]
        ref, first, _ = blocks[block]
        wide = lambda q: jnp.tile(cols[q, start : start + size, :], (1, seg // LANES))
        row = lambda q: ref[first + q : first + q + 1]
        dx = wide(0) - row(0)
        dy = wide(1) - row(1)
        span = (wide(2) * (row(2) * F32(-2.0)) + (wide(3) + row(3))) + (dx * dx + dy * dy)
        both = in_two(moment[step % 2, 0:size] * lax.rsqrt(span))
        high[step % 2, 0:size], low[step % 2, 0:size] = both

    def induce(step):
        block, start, size = spans[step]
        at = slice(start, start + size)
        both = lax.dot_general(cur[block % 2], high[step % 2, 0:size], nt, preferred_element_type=F32)
        rest = lax.dot_general(cur[block % 2, 0:COLS], low[step % 2, 0:size], nt, preferred_element_type=F32)
        voltage[:, at] += both[0:COLS] + both[COLS : 2 * COLS] + rest

    for step in range(steps + 2):
        if step >= 2:
            induce(step - 2)
        if step < steps:
            moments(step)
        if 1 <= step <= steps:
            kernel(step - 1)


def spread(turned, cols):
    for q in range(4):
        cols[q] = jnp.broadcast_to(turned[:, q : q + 1], cols.shape[1:])


def own_kernel(own, voltage, turned, left, cols, *buffers):
    geo = own[0:GEO]
    turned[...] = jnp.transpose(geo)
    left[...] = jnp.transpose(own_factor(geo))
    spread(turned[...], cols)
    voltage[...] = jnp.zeros_like(voltage)
    add_tiles(voltage, [(own, 0, None)], cols, left, *buffers)


def others_kernel(offsets, n_refs, flags, turned, left, before, *refs):
    found = [(ref, first) for ref in refs[:n_refs] for first in range(0, ref.shape[0], BLOCK)]
    voltage, cols, *buffers = refs[n_refs:]
    spread(turned[...], cols)
    voltage[...] = before[...]
    blocks = [
        (ref, first, flag_at(flags, offset(*place()))) for (ref, first), offset in zip(found, offsets, strict=True)
    ]
    add_tiles(voltage, blocks, cols, left, *buffers)


def scratch(seg):
    return [
        pltpu.VMEM((4, seg, LANES), F32),
        pltpu.VMEM((2, 96, seg), BF16),
        pltpu.VMEM((2, 2 * COLS, seg), BF16),
        pltpu.VMEM((2, ROWS, seg), F32),
        pltpu.VMEM((2, ROWS, seg), BF16),
        pltpu.VMEM((2, ROWS, seg), BF16),
    ]


def params(n, seg):
    return dict(
        compiler_params=pltpu.CompilerParams(vmem_limit_bytes=40 << 20),
        cost_estimate=pl.CostEstimate(
            flops=n * 6 * seg * seg * 192, bytes_accessed=n * BLOCK * seg * 4, transcendentals=n * seg * seg
        ),
    )


def own_tile(own):
    seg = own.shape[1]
    return pl.pallas_call(
        own_kernel,
        out_shape=(
            jax.ShapeDtypeStruct((COLS, seg), F32),
            jax.ShapeDtypeStruct((seg, GEO), F32),
            jax.ShapeDtypeStruct((seg, 96), BF16),
        ),
        in_specs=[VMEM],
        out_specs=(VMEM,) * 3,
        scratch_shapes=scratch(seg),
        **params(1, seg),
    )(own)


def other_tiles(flags, turned, left, voltage, blocks, offsets):
    seg = left.shape[0]
    return pl.pallas_call(
        functools.partial(others_kernel, offsets, len(blocks)),
        out_shape=jax.ShapeDtypeStruct((COLS, seg), F32),
        in_specs=[VMEM] * (4 + len(blocks)),
        out_specs=VMEM,
        scratch_shapes=scratch(seg),
        **params(len(offsets), seg),
    )(flags, turned, left, voltage, *blocks)


def sign(bit):
    return 1 - 2 * bit


def shards(geometry, currents, net_ids, pair_on):
    seg = geometry.shape[1]
    nets = net_ids[None, :]
    packed, flags = pl.pallas_call(
        pack_kernel,
        out_shape=(
            pltpu.VMEM((BLOCK, seg), F32),
            pltpu.VMEM((pair_on.shape[1], LANES), F32),
        ),
        in_specs=[VMEM] * 4,
        out_specs=(VMEM, VMEM),
    )(geometry, currents, nets, pair_on)
    n = lax.axis_size("blk")
    core, chip, half = place()
    within = swap(packed, lambda i: i ^ 4)
    across = swap(packed, lambda i: (((i - 4) % n ^ 4) + 4) % n)
    voltage, turned, left = own_tile(packed)
    across, within, voltage = lax.optimization_barrier((across, within, voltage))
    fourth = jnp.where(chip != half, across, within)
    second = swap(jnp.concatenate([packed, fourth], axis=0), lambda i: i ^ 2)
    voltage = other_tiles(
        flags,
        turned,
        left,
        voltage,
        [across, within],
        [lambda core, chip, half: -4 * sign(half), lambda core, chip, half: 4 * sign(half)],
    )
    second, voltage = lax.optimization_barrier((second, voltage))
    fourth = jnp.where(core != half, across, within)
    first = swap(jnp.concatenate([packed, fourth, second], axis=0), lambda i: i ^ 1)
    voltage = other_tiles(
        flags,
        turned,
        left,
        voltage,
        [second],
        [lambda core, chip, half: 2 * sign(chip), lambda core, chip, half: -2 * sign(chip)],
    )
    return other_tiles(
        flags,
        turned,
        left,
        voltage,
        [first],
        [
            lambda core, chip, half: sign(core),
            lambda core, chip, half: -3 * sign(core),
            lambda core, chip, half: sign(core) + 2 * sign(chip),
            lambda core, chip, half: sign(core) - 2 * sign(chip),
        ],
    )


def solution(mesh):
    return jax.shard_map(
        shards,
        mesh=mesh,
        in_specs=(P(None, "blk"), P(None, "blk"), P("blk"), P("blk", None)),
        out_specs=P(None, "blk"),
        check_vma=False,
    )
```
